256 devices in a mesh: req: 64 (over z, x, core), tp: 4 (over y).
Axes of the slice: x: 4, y: 4, z: 8, core: 2. Of those that a mesh axis runs over, the one named last changes fastest.
Arguments:
- tokens: bfloat16 [16384, 2048], P('req'), may hold values from -6 to 6
- segment_ids: int32 [16384], P('req'), may hold values from 0 to 15, never falling along the last dimension, each value on 1 to 8192 neighbouring positions
- mixer_gain: float32 [2048], replicated, may hold values from 0.1 to 1.9
- query_weight: bfloat16 [2048, 2048], P(None, 'tp'), may hold values from -0.5 to 0.5
- pair_weight: bfloat16 [2048, 512], P(None, 'tp'), may hold values from -3 to 3
- output_weight: bfloat16 [2048, 2048], P('tp'), may hold values from -0.125 to 0.125
- feed_gain: float32 [2048], replicated, may hold values from 0.1 to 1.9
- gate_weight: bfloat16 [2048, 2048], P(None, 'tp'), may hold values from -0.125 to 0.125
- up_weight: bfloat16 [2048, 2048], P(None, 'tp'), may hold values from -0.125 to 0.125
- down_weight: bfloat16 [2048, 2048], P('tp'), may hold values from -0.125 to 0.125
Outputs:
- block_output: bfloat16 [16384, 2048], P('req')
- key_values: bfloat16 [16384, 512], P('req', 'tp')
The draws below stay inside these ranges and needn't reach their ends.
All inputs are finite; a program needn't handle non-finite values.
Results may differ from the reference program's by a relative error of at most 0.015.
The reference program's roundings to bfloat16 on the way count: a program that leaves them out, or rounds other values in their place, can miss the bound.
Values may be sent and summed in bfloat16 or wider, within the bound.
A program may use at most 128 MiB of HBM per device.

```python
import math
import jax
import jax.numpy as jnp
import numpy as np
from jax import lax

D = 2048
H = 32
HD = 64
KVH = 4
FF = 2048
WINDOW = 2048
TOK_DEV = 256
TOKENS = 16384
SEGS = 16
MAXLEN = 8192
N_TP = 4


def weight_pair(key):
    base_key = jax.random.fold_in(key, 17)
    query_key = jax.random.fold_in(base_key, 1)
    value_key = jax.random.fold_in(base_key, 2)
    noise_key = jax.random.fold_in(base_key, 3)
    scale = D ** (-0.5)
    query_part = jnp.clip(jax.random.normal(query_key, (D, H * HD), jnp.float32), -4.0, 4.0) * scale
    value_part = jnp.clip(jax.random.normal(value_key, (D, KVH, 1, HD), jnp.float32), -4.0, 4.0) * scale
    noise = jnp.clip(jax.random.normal(noise_key, (D, KVH, 1, HD), jnp.float32), -4.0, 4.0) * scale
    key_part = noise
    pair_part = jnp.concatenate([key_part, value_part], axis=2).reshape(D, KVH * 2 * HD)
    return (query_part, pair_part)


def draw_query_weight(key, part):
    return weight_pair(key)[0].astype(jnp.bfloat16)


def draw_pair_weight(key, part):
    return weight_pair(key)[1].astype(jnp.bfloat16)


def levels(stream_key, dims, shards, low, top_value):
    level, own = 1.0, jax.random.fold_in(stream_key, 6)
    for dim, blocks in shards:
        steps = jnp.exp(jax.random.uniform(jax.random.fold_in(own, dim), (blocks,), jnp.float32, low / len(shards), top_value / len(shards)))
        level = level * jnp.repeat(steps, dims[dim] // blocks).reshape([-1 if axis == dim else 1 for axis in range(len(dims))])
    return level


def length_profile(number_of, total, reach, lean):
    weights = [(1 << 20) // math.isqrt(standing ** lean) + 1 for standing in range(2, number_of + 1)]
    spare, holding = total - reach - (number_of - 1), [1] * (number_of - 1)
    while spare > 0:
        free = [i for i in range(number_of - 1) if holding[i] < reach]
        whole, budget = sum([weights[i] for i in free]), spare
        for i in free:
            addition = min(reach - holding[i], max(1, budget * weights[i] // whole), spare)
            holding[i] = holding[i] + addition
            spare = spare - addition
    return np.array([reach] + holding)


def uneven(key, number_of, total, reach, slope):
    if number_of == 2:
        one = jax.random.randint(key, (), max(1, total - reach), min(reach, total - 1) + 1)
        return jnp.stack([one, total - one])
    lengths = jnp.asarray(length_profile(number_of, total, reach, slope), jnp.int32)
    couples = (number_of - 1) // 2
    source_of, taker = lengths[1:1 + 2 * couples:2], lengths[2:2 + 2 * couples:2]
    room = jnp.minimum(source_of - 1, reach - taker)
    shifted = jax.random.randint(jax.random.fold_in(key, 1), (couples,), 0, 1 << 20) % (room + 1)
    lengths = lengths.at[1:1 + 2 * couples:2].set(source_of - shifted).at[2:2 + 2 * couples:2].set(taker + shifted)
    return lengths[jax.random.permutation(jax.random.fold_in(key, 2), number_of)]


def scatter_about(key, shape, scale, most, shards=(), held_as=jnp.bfloat16):
    level = levels(key, shape, shards, -0.22, 0.18) if shards else 1.0
    array = jax.random.normal(key, shape, jnp.float32) * scale * level
    return jnp.minimum(jnp.maximum(array, -most), most).astype(held_as)


def setup_inputs(seed: int = 0) -> dict:
    key_of = jax.random.split(jax.random.key(seed), 11)
    return {
        "tokens": scatter_about(key_of[0], (TOKENS, D), 1.0, 6.0, ((0, 64),)),
        "segment_ids": jnp.searchsorted(jnp.cumsum(uneven(key_of[1], SEGS, TOKENS, MAXLEN, 2)), jnp.arange(TOKENS), side="right").astype(jnp.int32),
        "mixer_gain": jnp.clip(1.0 + 0.18 * jax.random.normal(key_of[2], (D,), jnp.float32), 0.1, 1.9),
        "query_weight": draw_query_weight(jax.random.fold_in(key_of[10], 71), 0),
        "pair_weight": draw_pair_weight(jax.random.fold_in(key_of[10], 71), 0),
        "output_weight": scatter_about(key_of[5], (H * HD, D), (H * HD) ** -0.5, 0.125, ((0, 4),)),
        "feed_gain": jnp.clip(1.0 + 0.18 * jax.random.normal(key_of[6], (D,), jnp.float32), 0.1, 1.9),
        "gate_weight": scatter_about(key_of[7], (D, FF), D ** -0.5, 0.125, ((1, 4),)),
        "up_weight": scatter_about(key_of[8], (D, FF), D ** -0.5, 0.125, ((1, 4),)),
        "down_weight": scatter_about(key_of[9], (FF, D), FF ** -0.5, 0.125, ((0, 4),)),
    }


epsilon = 1e-05

def rms_scale(matrix, gain):
    matrix = matrix.astype(jnp.float32)
    mean_square = lax.optimization_barrier(jnp.mean(matrix * matrix, axis=-1, keepdims=True))
    return matrix * lax.rsqrt(mean_square + epsilon) * gain.astype(jnp.float32)

def rotary(head_data, position):
    half_width = head_data.shape[-1] // 2
    frequency = jnp.exp(-math.log(10000.0) * jnp.arange(half_width, dtype=jnp.float32) / half_width)
    angles = position.astype(jnp.float32)[:, None] * frequency[None, :]
    cosine = jnp.cos(angles)[:, None, :]
    sine_part = jnp.sin(angles)[:, None, :]
    front_half = head_data[..., :half_width]
    back_half = head_data[..., half_width:]
    return jnp.concatenate([front_half * cosine - back_half * sine_part, back_half * cosine + front_half * sine_part], axis=-1)

def reference(tokens, segment_ids, mixer_gain, query_weight, pair_weight, output_weight, feed_gain, gate_weight, up_weight, down_weight):
    position = jnp.arange(TOKENS, dtype=jnp.int32)
    normed = rms_scale(tokens, mixer_gain).astype(jnp.bfloat16)
    queries = jnp.dot(normed, query_weight, preferred_element_type=jnp.float32).reshape(TOKENS, H, HD)
    queries = rotary(queries, position).astype(jnp.bfloat16)
    pair_rows = jnp.dot(normed, pair_weight, preferred_element_type=jnp.float32).reshape(TOKENS, KVH, 2, HD)
    rotated_keys = rotary(pair_rows[:, :, 0], position)
    key_values = jnp.stack([rotated_keys, pair_rows[:, :, 1]], axis=2).astype(jnp.bfloat16)
    segment_list = jnp.arange(SEGS, dtype=jnp.int32)
    firsts = lax.optimization_barrier(jnp.min(jnp.where(segment_ids[None, :] == segment_list[:, None], position[None, :], TOKENS), axis=1)).astype(jnp.int32)
    starts = firsts[segment_ids]
    padded = jnp.concatenate([jnp.zeros((WINDOW, KVH, 2, HD), jnp.bfloat16), key_values], axis=0)
    group_size = H // KVH
    key_count = WINDOW + TOK_DEV

    def attend_block(block_index):
        first_row = block_index * TOK_DEV
        grouped = lax.dynamic_slice_in_dim(queries, first_row, TOK_DEV, 0).astype(jnp.float32).reshape(TOK_DEV, KVH, group_size, HD)
        block_pairs = lax.dynamic_slice_in_dim(padded, first_row, key_count, 0).astype(jnp.float32)
        query_position = first_row + jnp.arange(TOK_DEV, dtype=jnp.int32)
        key_position = first_row - WINDOW + jnp.arange(key_count, dtype=jnp.int32)
        row_starts = lax.dynamic_slice_in_dim(starts, first_row, TOK_DEV, 0)
        scores = jnp.einsum('qcgd,kcd->cgqk', grouped, block_pairs[:, :, 0]) * HD ** (-0.5)
        allowed = (key_position[None, :] >= row_starts[:, None]) & (key_position[None, :] <= query_position[:, None]) & (key_position[None, :] > query_position[:, None] - WINDOW)
        scores = jnp.where(allowed[None, None], scores, -jnp.inf)
        row_max = lax.optimization_barrier(jnp.max(scores, axis=-1, keepdims=True))
        weights = jnp.exp(scores - row_max)
        weights = (weights / lax.optimization_barrier(jnp.sum(weights, axis=-1, keepdims=True))).astype(jnp.bfloat16)
        mixed_heads = jnp.einsum('cgqk,kcd->qcgd', weights.astype(jnp.float32), block_pairs[:, :, 1])
        return mixed_heads.reshape(TOK_DEV, H * HD).astype(jnp.bfloat16)
    heads_out = lax.map(attend_block, jnp.arange(TOKENS // TOK_DEV, dtype=jnp.int32)).reshape(TOKENS, H * HD)
    group_width = H * HD // N_TP
    attention = jnp.zeros((TOKENS, D), jnp.float32)
    for group_index in range(N_TP):
        partial_value = jnp.dot(heads_out[:, group_index * group_width:(group_index + 1) * group_width], output_weight[group_index * group_width:(group_index + 1) * group_width], preferred_element_type=jnp.float32)
        attention = attention + lax.optimization_barrier(partial_value.astype(jnp.bfloat16)).astype(jnp.float32)
    residual = tokens.astype(jnp.float32) + attention
    normed_mid = rms_scale(residual, feed_gain).astype(jnp.bfloat16)
    gate_rows = jnp.dot(normed_mid, gate_weight, preferred_element_type=jnp.float32)
    up_rows = jnp.dot(normed_mid, up_weight, preferred_element_type=jnp.float32)
    hidden = (jax.nn.silu(gate_rows) * up_rows).astype(jnp.bfloat16)
    unit_width = FF // N_TP
    feed_out = jnp.zeros((TOKENS, D), jnp.float32)
    for group_index in range(N_TP):
        partial_value = jnp.dot(hidden[:, group_index * unit_width:(group_index + 1) * unit_width], down_weight[group_index * unit_width:(group_index + 1) * unit_width], preferred_element_type=jnp.float32)
        feed_out = feed_out + lax.optimization_barrier(partial_value.astype(jnp.bfloat16)).astype(jnp.float32)
    block_output = (residual + feed_out).astype(jnp.bfloat16)
    return (block_output, key_values.reshape(TOKENS, KVH * 2 * HD))
```

```python
import math

import jax
import jax.numpy as jnp
import numpy as np
from jax import lax
from jax.experimental import pallas as pl
from jax.experimental.pallas import tpu as pltpu
from jax.sharding import PartitionSpec as P

MESH = pl.DeviceIdType.MESH
F32 = jnp.float32
BF16 = jnp.bfloat16
NEG = -1e30
EPS = 1e-05

T = 256
D = 2048
REQ = 64
TP = 4
HEADS = 8
HD = 64
C = 512
F = 512
CH = T // TP
HALF = D // 2
BLOCKS = 8
KROWS = T + 16


def rope_tables():
    freq = np.exp(-math.log(10000.0) * np.arange(32, dtype=np.float32) / np.float32(32)).astype(np.float32)
    freq = np.tile(freq.astype(np.float64), 4)[None, :]
    base = (np.arange(REQ) * T)[:, None] * freq
    inner = np.arange(T)[:, None] * freq
    base = np.stack([np.cos(base), np.sin(base)]).astype(np.float32)
    inner = np.stack([np.cos(inner), np.sin(inner)]).astype(np.float32)
    return base, inner


def iota(shape, dim):
    return lax.broadcasted_iota(jnp.int32, shape, dim)


def kernel(
    tok_h, seg_ref, g1_ref, g2_ref, base_ref, inner_ref,
    qw_h, pw_h, ow_h, gw_h, uw_h, dw_h,
    out_h, kvout_h,
    tok, normed, pw, qw, ow, gw, uw, dw,
    kvb, kT, vx, qa, S, M, Pm, ho, hid, sb, rb, own, own2, res, mid, outb,
    ld, kvo, oo, dsend, drecv, fsend, frecv, rsend, rrecv, asend, arecv,
):
    r = lax.axis_index("req")
    y = lax.axis_index("tp")
    core = lax.rem(r, 2)
    partner = r + 1 - 2 * core
    right = lax.rem(y + 1, TP)
    left = lax.rem(y + 3, TP)
    opp = lax.rem(y + 2, TP)

    barrier = pltpu.get_barrier_semaphore()
    for k in range(1, 5):
        pl.semaphore_signal(
            barrier, inc=1, device_id=(lax.rem(r + REQ - 2 * k, REQ), y), device_id_type=MESH
        )
    pl.semaphore_signal(barrier, inc=1, device_id=(partner, y), device_id_type=MESH)
    pl.semaphore_signal(barrier, inc=1, device_id=(r, right), device_id_type=MESH)
    pl.semaphore_signal(barrier, inc=1, device_id=(r, left), device_id_type=MESH)

    def load(i, src, dst):
        return pltpu.make_async_copy(src, dst, ld.at[i])

    loads = [
        load(i, s, d)
        for i, (s, d) in enumerate(
            [(tok_h, tok), (pw_h, pw), (qw_h, qw), (ow_h, ow), (gw_h, gw), (uw_h, uw), (dw_h, dw)]
        )
    ]
    for c in loads[:3]:
        c.start()

    ca, sa = base_ref[0, pl.ds(r, 1), :], base_ref[1, pl.ds(r, 1), :]
    cb, sn = inner_ref[0], inner_ref[1]
    cos = ca * cb - sa * sn
    sin = sa * cb + ca * sn
    lane = iota((T, 128), 1)
    first = lax.rem(lane, 64) < 32
    s_up = jnp.where(first, -sin, 0.0)
    s_dn = jnp.where(first, 0.0, sin)

    def rotate(x, c, su, sd):
        return x * c + pltpu.roll(x, 96, 1) * su + pltpu.roll(x, 32, 1) * sd

    seg_row = seg_ref[...].astype(F32)
    seg_col = jnp.broadcast_to(seg_row, (128, T)).T
    loads[0].wait()

    def norm_rows(i, carry):
        rows = pl.ds(pl.multiple_of(i * 16, 16), 16)
        x = tok[rows, :].astype(F32)
        ms = jnp.mean(x * x, axis=-1, keepdims=True)
        normed[rows, :] = (x * lax.rsqrt(ms + EPS) * g1_ref[...]).astype(BF16)
        return carry

    lax.fori_loop(0, T // 16, norm_rows, 0, unroll=2)

    loads[1].wait()
    kv = jnp.dot(normed[...], pw[...], preferred_element_type=F32)
    isk = lane < 64
    kv = rotate(kv, jnp.where(isk, cos, 1.0), jnp.where(isk, s_up, 0.0), jnp.where(isk, s_dn, 0.0))
    kvb[0, 0:T, :] = kv.astype(BF16)
    srow = iota((16, 128), 0)
    kvb[0, T:KROWS, :] = jnp.where(
        srow == 0, seg_row[:, :128], jnp.where(srow == 1, seg_row[:, 128:], 0.0)
    ).astype(BF16)

    pl.semaphore_wait(barrier, 7)

    def direct(k):
        return pltpu.make_async_remote_copy(
            src_ref=kvb.at[0], dst_ref=kvb.at[2 * k],
            send_sem=dsend.at[k - 1], recv_sem=drecv.at[k - 1],
            device_id=(lax.rem(r + 2 * k, REQ), y), device_id_type=MESH,
        )

    def forward(j, src):
        return pltpu.make_async_remote_copy(
            src_ref=kvb.at[src], dst_ref=kvb.at[2 * j + 1],
            send_sem=fsend.at[j], recv_sem=frecv.at[j],
            device_id=(partner, y), device_id_type=MESH,
        )

    for k in (4, 3, 2, 1):
        direct(k).start()

    @pl.when(core == 0)
    def _():
        forward(0, 0).start()

    kv_copy = pltpu.make_async_copy(kvb.at[0, 0:T, :], kvout_h, kvo)
    kv_copy.start()
    for c in loads[3:]:
        c.start()

    loads[2].wait()
    qpen = jnp.where((lane - 64).astype(F32) == seg_col, NEG, 0.0)
    qpen = jnp.where(lane < 80, qpen, 0.0)
    for n in range(2):
        q4 = jnp.dot(normed[...], qw[:, n * 256:(n + 1) * 256], preferred_element_type=F32)
        for i in range(2):
            q2 = rotate(q4[:, i * 128:(i + 1) * 128], cos, s_up, s_dn) * (HD ** -0.5)
            h = n * 4 + i * 2
            qa[h] = jnp.where(isk, q2, qpen).astype(BF16)
            qa[h + 1] = jnp.where(isk, pltpu.roll(q2, 64, 1), qpen).astype(BF16)

    def prepare(d):
        kv = kvb[d, 0:T, :].astype(F32)
        ids = kvb[d, T:KROWS, :].astype(F32)
        ids = jnp.concatenate([ids[0:1], ids[1:2]], axis=1) + jnp.where(r >= d, 0.0, 100.0)
        row = iota((128, T), 0)
        differs = jnp.where((row - 64).astype(F32) == ids, 0.0, 1.0)
        kT[d] = jnp.where(row < 64, kv.T, jnp.where(row < 80, differs, 0.0)).astype(BF16)
        vx[d * T:(d + 1) * T, :] = jnp.where(isk, pltpu.roll(kv, 64, 1), 1.0).astype(BF16)

    def score(d):
        def body(h, carry):
            s = jnp.dot(qa[h], kT[d], preferred_element_type=F32)
            at = (d % BLOCKS) * T
            if d in (0, BLOCKS):
                seen = iota((T, T), 1) <= iota((T, T), 0)
                s = jnp.where(seen, s if d == 0 else S[h, :, 0:T], NEG if d == 0 else s)
            S[h, :, at:at + T] = s
            top = jnp.maximum(s[:, :128], s[:, 128:])
            M[h] = top if d == 0 else jnp.maximum(M[h], top)
            return carry

        lax.fori_loop(0, HEADS, body, 0)

    prepare(0)
    score(0)
    for k in range(1, 5):
        direct(k).wait_recv()

        @pl.when(core == 1)
        def _():
            forward(k - 1, 2 * k).start()

        if k < 4:
            @pl.when(core == 0)
            def _():
                forward(k, 2 * k).start()

        prepare(2 * k)
        score(2 * k)
        forward(k - 1, 0).wait_recv()
        prepare(2 * k - 1)
        score(2 * k - 1)

    loads[3].wait()

    def attend(chunk):
        r0 = pl.multiple_of(chunk * CH, CH)
        rows = pl.ds(r0, CH)

        def head(h, carry):
            m = jnp.max(M[h, rows, :], axis=1, keepdims=True)
            to = pl.ds(pl.multiple_of(h * CH, CH), CH)
            for b in range(BLOCKS):
                p = jnp.exp(S[h, rows, b * T:(b + 1) * T] - m)
                if b == 0:
                    seen = iota((CH, T), 1) <= iota((CH, T), 0) + r0
                    Pm[to, BLOCKS * T:(BLOCKS + 1) * T] = jnp.where(seen, 0.0, p).astype(BF16)
                    p = jnp.where(seen, p, 0.0)
                Pm[to, b * T:(b + 1) * T] = p.astype(BF16)
            return carry

        lax.fori_loop(0, HEADS, head, 0)
        low = iota((CH, 128), 1) < 64
        for n in range(2):
            o = jnp.dot(Pm[n * 256:(n + 1) * 256, :], vx[...], preferred_element_type=F32)
            o = o / pltpu.roll(o, 64, 1)
            for i in range(2):
                even, odd = o[i * 128:i * 128 + 64], o[i * 128 + 64:i * 128 + 128]
                at = (n * 2 + i) * 128
                ho[:, at:at + 128] = jnp.where(low, even, pltpu.roll(odd, 64, 1)).astype(BF16)

    def project(x, w, n):
        return jnp.dot(x[...], w[:, n * HALF:(n + 1) * HALF], preferred_element_type=F32).astype(BF16)

    def rs(round_, i):
        at = round_ * 6 + i
        return pltpu.make_async_remote_copy(
            src_ref=sb.at[at], dst_ref=rb.at[at], send_sem=rsend.at[at], recv_sem=rrecv.at[at],
            device_id=(r, right if i < 3 else left), device_id_type=MESH,
        )

    attend(opp)
    sb[0] = project(ho, ow, 0)
    rs(0, 0).start()
    sb[3] = project(ho, ow, 1)
    rs(0, 3).start()
    attend(right)
    sb[2] = project(ho, ow, 1)
    rs(0, 2).start()
    part = project(ho, ow, 0)
    rs(0, 0).wait_recv()
    sb[1] = (part.astype(F32) + rb[0].astype(F32)).astype(BF16)
    rs(0, 1).start()
    attend(left)
    sb[5] = project(ho, ow, 0)
    rs(0, 5).start()
    part = project(ho, ow, 1)
    rs(0, 3).wait_recv()
    sb[4] = (part.astype(F32) + rb[3].astype(F32)).astype(BF16)
    rs(0, 4).start()
    attend(y)
    for n in range(2):
        own[:, n * HALF:(n + 1) * HALF] = project(ho, ow, n)

    mine = pl.ds(pl.multiple_of(y * CH, CH), CH)
    for i in (1, 2, 4, 5):
        rs(0, i).wait_recv()

    def mix(i, carry):
        at = pl.multiple_of(i * 16, 16)
        rows = pl.ds(at, 16)
        x = tok[pl.ds(pl.multiple_of(y * CH + i * 16, 16), 16), :].astype(F32)
        o = own[rows, :].astype(F32)
        add_a = rb[1, rows, :].astype(F32) + rb[5, rows, :].astype(F32)
        add_b = rb[2, rows, :].astype(F32) + rb[4, rows, :].astype(F32)
        x = x + o + jnp.concatenate([add_a, add_b], axis=1)
        res[rows, :] = x
        ms = jnp.mean(x * x, axis=-1, keepdims=True)
        mid[pl.ds(pl.multiple_of(y * CH + i * 16, 16), 16), :] = (
            x * lax.rsqrt(ms + EPS) * g2_ref[...]
        ).astype(BF16)
        return carry

    lax.fori_loop(0, CH // 16, mix, 0)

    def ag(round_, i, buf):
        at = round_ * 6 + i
        chunk = (y, y, left, y, y, right)[i]
        half = (0, 1, 0, 1, 0, 1)[i]
        where = buf.at[pl.ds(pl.multiple_of(chunk * CH, CH), CH), pl.ds(half * HALF, HALF)]
        return pltpu.make_async_remote_copy(
            src_ref=where, dst_ref=where, send_sem=asend.at[at], recv_sem=arecv.at[at],
            device_id=(r, right if i < 3 else left), device_id_type=MESH,
        )

    def gather_start(round_, buf):
        for i in (0, 3, 1, 4):
            ag(round_, i, buf).start()

    def gather_pass(round_, buf):
        ag(round_, 0, buf).wait_recv()
        ag(round_, 2, buf).start()
        ag(round_, 3, buf).wait_recv()
        ag(round_, 5, buf).start()

    gather_start(0, mid)
    for c in loads[4:]:
        c.wait()

    def feed(chunk):
        x = mid[pl.ds(pl.multiple_of(chunk * CH, CH), CH), :]
        for n in range(2):
            cols = slice(n * 256, (n + 1) * 256)
            g = jnp.dot(x, gw[:, cols], preferred_element_type=F32)
            u = jnp.dot(x, uw[:, cols], preferred_element_type=F32)
            hid[:, cols] = (g / (1.0 + jnp.exp(-g)) * u).astype(BF16)

    feed(y)
    for n in range(2):
        own2[:, n * HALF:(n + 1) * HALF] = project(hid, dw, n)
    gather_pass(0, mid)
    ag(0, 1, mid).wait_recv()
    feed(left)
    sb[11] = project(hid, dw, 0)
    rs(1, 5).start()
    sb[10] = project(hid, dw, 1)
    ag(0, 4, mid).wait_recv()
    feed(right)
    sb[8] = project(hid, dw, 1)
    rs(1, 2).start()
    sb[7] = project(hid, dw, 0)
    ag(0, 2, mid).wait_recv()
    ag(0, 5, mid).wait_recv()
    feed(opp)
    sb[6] = project(hid, dw, 0)
    rs(1, 0).start()
    sb[9] = project(hid, dw, 1)
    rs(1, 3).start()
    rs(1, 0).wait_recv()
    sb[7] = (sb[7].astype(F32) + rb[6].astype(F32)).astype(BF16)
    rs(1, 1).start()
    rs(1, 3).wait_recv()
    sb[10] = (sb[10].astype(F32) + rb[9].astype(F32)).astype(BF16)
    rs(1, 4).start()
    for i in (1, 2, 4, 5):
        rs(1, i).wait_recv()

    def finish(i, carry):
        rows = pl.ds(pl.multiple_of(i * 16, 16), 16)
        o = own2[rows, :].astype(F32)
        add_a = rb[7, rows, :].astype(F32) + rb[11, rows, :].astype(F32)
        add_b = rb[8, rows, :].astype(F32) + rb[10, rows, :].astype(F32)
        x = res[rows, :] + (o + jnp.concatenate([add_a, add_b], axis=1))
        outb[pl.ds(pl.multiple_of(y * CH + i * 16, 16), 16), :] = x.astype(BF16)
        return carry

    lax.fori_loop(0, CH // 16, finish, 0)
    gather_start(1, outb)

    def put(i, chunk):
        rows = pl.ds(pl.multiple_of(chunk * CH, CH), CH)
        return pltpu.make_async_copy(outb.at[rows, :], out_h.at[rows, :], oo.at[i])

    put(0, y).start()
    gather_pass(1, outb)
    ag(1, 1, outb).wait_recv()
    put(1, left).start()
    ag(1, 4, outb).wait_recv()
    put(2, right).start()
    ag(1, 2, outb).wait_recv()
    ag(1, 5, outb).wait_recv()
    put(3, opp).start()

    for k in range(1, 5):
        direct(k).wait_send()
        forward(k - 1, 0).wait_send()
    for i in range(6):
        rs(0, i).wait_send()
        rs(1, i).wait_send()
        ag(0, i, mid).wait_send()
        ag(1, i, outb).wait_send()
    kv_copy.wait()
    for i, chunk in enumerate((y, left, right, opp)):
        put(i, chunk).wait()


def body(tokens, segment_ids, mixer_gain, query_weight, pair_weight, output_weight, feed_gain,
         gate_weight, up_weight, down_weight):
    base, inner = rope_tables()
    hbm = pl.BlockSpec(memory_space=pl.ANY)
    vm = pl.BlockSpec(memory_space=pltpu.VMEM)
    dma = pltpu.SemaphoreType.DMA
    return pl.pallas_call(
        kernel,
        out_shape=(
            jax.ShapeDtypeStruct((T, D), BF16),
            jax.ShapeDtypeStruct((T, 128), BF16),
        ),
        in_specs=[hbm, vm, vm, vm, vm, vm] + [hbm] * 6,
        out_specs=(hbm, hbm),
        scratch_shapes=[
            pltpu.VMEM((T, D), BF16),
            pltpu.VMEM((T, D), BF16),
            pltpu.VMEM((D, 128), BF16),
            pltpu.VMEM((D, C), BF16),
            pltpu.VMEM((C, D), BF16),
            pltpu.VMEM((D, F), BF16),
            pltpu.VMEM((D, F), BF16),
            pltpu.VMEM((F, D), BF16),
            pltpu.VMEM((BLOCKS + 1, KROWS, 128), BF16),
            pltpu.VMEM((BLOCKS + 1, 128, T), BF16),
            pltpu.VMEM(((BLOCKS + 1) * T, 128), BF16),
            pltpu.VMEM((HEADS, T, 128), BF16),
            pltpu.VMEM((HEADS, T, BLOCKS * T), F32),
            pltpu.VMEM((HEADS, T, 128), F32),
            pltpu.VMEM((HEADS * CH, (BLOCKS + 1) * T), BF16),
            pltpu.VMEM((CH, C), BF16),
            pltpu.VMEM((CH, F), BF16),
            pltpu.VMEM((12, CH, HALF), BF16),
            pltpu.VMEM((12, CH, HALF), BF16),
            pltpu.VMEM((CH, D), BF16),
            pltpu.VMEM((CH, D), BF16),
            pltpu.VMEM((CH, D), F32),
            pltpu.VMEM((T, D), BF16),
            pltpu.VMEM((T, D), BF16),
            dma((7,)), dma, dma((4,)),
            dma((4,)), dma((4,)), dma((4,)), dma((4,)),
            dma((12,)), dma((12,)), dma((12,)), dma((12,)),
        ],
        compiler_params=pltpu.CompilerParams(
            collective_id=0, has_side_effects=True, vmem_limit_bytes=64 * 1024 * 1024 - 65536
        ),
        name="block",
    )(
        tokens, segment_ids.reshape(1, T), mixer_gain.reshape(1, D), feed_gain.reshape(1, D),
        jnp.asarray(base), jnp.asarray(inner),
        query_weight, pair_weight, output_weight, gate_weight, up_weight, down_weight,
    )


def solution(mesh):
    return jax.shard_map(
        body,
        mesh=mesh,
        in_specs=(
            P("req", None),
            P("req"),
            P(),
            P(None, "tp"),
            P(None, "tp"),
            P("tp", None),
            P(),
            P(None, "tp"),
            P(None, "tp"),
            P("tp", None),
        ),
        out_specs=(P("req", None), P("req", "tp")),
        check_vma=False,
    )
```

```python
import math

import jax
import jax.numpy as jnp
import numpy as np
from jax import lax
from jax.experimental import pallas as pl
from jax.experimental.pallas import tpu as pltpu
from jax.sharding import PartitionSpec as P

MESH = pl.DeviceIdType.MESH
F32 = jnp.float32
BF16 = jnp.bfloat16
NEG = -1e30
EPS = 1e-05

T = 256
D = 2048
REQ = 64
TP = 4
HEADS = 8
HD = 64
C = 512
F = 512
CH = T // TP
HALF = D // 2
BLOCKS = 8
KROWS = T + 16


def rope_tables():
    freq = np.exp(-math.log(10000.0) * np.arange(32, dtype=np.float32) / np.float32(32)).astype(np.float32)
    freq = np.tile(freq.astype(np.float64), 4)[None, :]
    base = (np.arange(REQ) * T)[:, None] * freq
    inner = np.arange(T)[:, None] * freq
    base = np.stack([np.cos(base), np.sin(base)]).astype(np.float32)
    inner = np.stack([np.cos(inner), np.sin(inner)]).astype(np.float32)
    return base, inner


def iota(shape, dim):
    return lax.broadcasted_iota(jnp.int32, shape, dim)


def kernel(
    tok_h, seg_ref, g1_ref, g2_ref, base_ref, inner_ref,
    qw_h, pw_h, ow_h, gw_h, uw_h, dw_h,
    out_h, kvout_h,
    tok, normed, pw, qw, ow, gw, uw, dw,
    kvb, kT, vx, qa, S, M, Pm, ho, sb, rb, own, own2, res, mid, outb,
    ld, kvo, oo, dsend, drecv, fsend, frecv, rsend, rrecv, asend, arecv,
):
    r = lax.axis_index("req")
    y = lax.axis_index("tp")
    core = lax.rem(r, 2)
    partner = r + 1 - 2 * core
    right = lax.rem(y + 1, TP)
    left = lax.rem(y + 3, TP)
    opp = lax.rem(y + 2, TP)

    barrier = pltpu.get_barrier_semaphore()
    for k in range(1, 5):
        pl.semaphore_signal(
            barrier, inc=1, device_id=(lax.rem(r + REQ - 2 * k, REQ), y), device_id_type=MESH
        )
    pl.semaphore_signal(barrier, inc=1, device_id=(partner, y), device_id_type=MESH)
    pl.semaphore_signal(barrier, inc=1, device_id=(r, right), device_id_type=MESH)
    pl.semaphore_signal(barrier, inc=1, device_id=(r, left), device_id_type=MESH)

    def load(i, src, dst):
        return pltpu.make_async_copy(src, dst, ld.at[i])

    loads = [
        load(i, s, d)
        for i, (s, d) in enumerate(
            [(tok_h, tok), (pw_h, pw), (qw_h, qw), (ow_h, ow), (gw_h, gw), (uw_h, uw), (dw_h, dw)]
        )
    ]
    for c in loads[:3]:
        c.start()

    ca, sa = base_ref[0, pl.ds(r, 1), :], base_ref[1, pl.ds(r, 1), :]
    cb, sn = inner_ref[0], inner_ref[1]
    cos = ca * cb - sa * sn
    sin = sa * cb + ca * sn
    lane = iota((T, 128), 1)
    first = lax.rem(lane, 64) < 32
    s_up = jnp.where(first, -sin, 0.0)
    s_dn = jnp.where(first, 0.0, sin)

    def rotate(x, c, su, sd):
        return x * c + pltpu.roll(x, 96, 1) * su + pltpu.roll(x, 32, 1) * sd

    seg_row = seg_ref[...].astype(F32)
    seg_col = jnp.broadcast_to(seg_row, (128, T)).T
    loads[0].wait()

    def norm_rows(i, carry):
        rows = pl.ds(pl.multiple_of(i * 16, 16), 16)
        x = tok[rows, :].astype(F32)
        ms = jnp.mean(x * x, axis=-1, keepdims=True)
        normed[rows, :] = (x * lax.rsqrt(ms + EPS) * g1_ref[...]).astype(BF16)
        return carry

    lax.fori_loop(0, T // 16, norm_rows, 0, unroll=2)

    loads[1].wait()
    kv = jnp.dot(normed[...], pw[...], preferred_element_type=F32)
    isk = lane < 64
    kv = rotate(kv, jnp.where(isk, cos, 1.0), jnp.where(isk, s_up, 0.0), jnp.where(isk, s_dn, 0.0))
    kvb[0, 0:T, :] = kv.astype(BF16)
    srow = iota((16, 128), 0)
    kvb[0, T:KROWS, :] = jnp.where(
        srow == 0, seg_row[:, :128], jnp.where(srow == 1, seg_row[:, 128:], 0.0)
    ).astype(BF16)

    pl.semaphore_wait(barrier, 7)

    def direct(k):
        return pltpu.make_async_remote_copy(
            src_ref=kvb.at[0], dst_ref=kvb.at[2 * k],
            send_sem=dsend.at[k - 1], recv_sem=drecv.at[k - 1],
            device_id=(lax.rem(r + 2 * k, REQ), y), device_id_type=MESH,
        )

    def forward(j, src):
        return pltpu.make_async_remote_copy(
            src_ref=kvb.at[src], dst_ref=kvb.at[2 * j + 1],
            send_sem=fsend.at[j], recv_sem=frecv.at[j],
            device_id=(partner, y), device_id_type=MESH,
        )

    for k in range(1, 5):
        direct(k).start()

    @pl.when(core == 0)
    def _():
        forward(0, 0).start()

    kv_copy = pltpu.make_async_copy(kvb.at[0, 0:T, :], kvout_h, kvo)
    kv_copy.start()
    for c in loads[3:]:
        c.start()

    loads[2].wait()
    qpen = jnp.where((lane - 64).astype(F32) == seg_col, NEG, 0.0)
    qpen = jnp.where(lane < 80, qpen, 0.0)
    for n in range(2):
        q4 = jnp.dot(normed[...], qw[:, n * 256:(n + 1) * 256], preferred_element_type=F32)
        for i in range(2):
            q2 = rotate(q4[:, i * 128:(i + 1) * 128], cos, s_up, s_dn) * (HD ** -0.5)
            h = n * 4 + i * 2
            qa[h] = jnp.where(isk, q2, qpen).astype(BF16)
            qa[h + 1] = jnp.where(isk, pltpu.roll(q2, 64, 1), qpen).astype(BF16)

    def prepare(d):
        kv = kvb[d, 0:T, :].astype(F32)
        ids = kvb[d, T:KROWS, :].astype(F32)
        ids = jnp.concatenate([ids[0:1], ids[1:2]], axis=1) + jnp.where(r >= d, 0.0, 100.0)
        row = iota((128, T), 0)
        differs = jnp.where((row - 64).astype(F32) == ids, 0.0, 1.0)
        kT[d] = jnp.where(row < 64, kv.T, jnp.where(row < 80, differs, 0.0)).astype(BF16)
        vx[d * T:(d + 1) * T, :] = jnp.where(isk, pltpu.roll(kv, 64, 1), 1.0).astype(BF16)

    def top(d):
        prepare(d)

        def body(h, carry):
            s = jnp.dot(qa[h], kT[d], preferred_element_type=F32)
            at = (d % BLOCKS) * T
            if d in (0, BLOCKS):
                seen = iota((T, T), 1) <= iota((T, T), 0)
                s = jnp.where(seen, s if d == 0 else S[h, :, 0:T], NEG if d == 0 else s)
            S[h, :, at:at + T] = s
            top = jnp.maximum(s[:, :128], s[:, 128:])
            M[h] = top if d == 0 else jnp.maximum(M[h], top)
            return carry

        lax.fori_loop(0, HEADS, body, 0)

    def arrive(k):
        direct(k).wait_recv()

        @pl.when(core == 1)
        def _():
            forward(k - 1, 2 * k).start()

        if k < 4:
            @pl.when(core == 0)
            def _():
                forward(k, 2 * k).start()

    top(0)
    arrive(1)
    top(2)
    for k in range(2, 5):
        arrive(k)
        forward(k - 2, 0).wait_recv()
        top(2 * k - 3)
        top(2 * k)
    forward(3, 0).wait_recv()
    top(7)

    loads[3].wait()

    def attend(chunk):
        r0 = pl.multiple_of(chunk * CH, CH)
        rows = pl.ds(r0, CH)

        def head(h, carry):
            m = jnp.max(M[h, rows, :], axis=1, keepdims=True)
            to = pl.ds(pl.multiple_of(h * CH, CH), CH)
            for b in range(BLOCKS):
                p = jnp.exp(S[h, rows, b * T:(b + 1) * T] - m)
                if b == 0:
                    seen = iota((CH, T), 1) <= iota((CH, T), 0) + r0
                    Pm[to, BLOCKS * T:(BLOCKS + 1) * T] = jnp.where(seen, 0.0, p).astype(BF16)
                    p = jnp.where(seen, p, 0.0)
                Pm[to, b * T:(b + 1) * T] = p.astype(BF16)
            return carry

        lax.fori_loop(0, HEADS, head, 0)
        low = iota((CH, 128), 1) < 64
        for n in range(2):
            o = jnp.dot(Pm[n * 256:(n + 1) * 256, :], vx[...], preferred_element_type=F32)
            o = o / pltpu.roll(o, 64, 1)
            for i in range(2):
                even, odd = o[i * 128:i * 128 + 64], o[i * 128 + 64:i * 128 + 128]
                at = (n * 2 + i) * 128
                ho[:, at:at + 128] = jnp.where(low, even, pltpu.roll(odd, 64, 1)).astype(BF16)

    def project(x, w, n):
        return jnp.dot(x[...], w[:, n * HALF:(n + 1) * HALF], preferred_element_type=F32).astype(BF16)

    def rs(round_, i):
        at = round_ * 6 + i
        return pltpu.make_async_remote_copy(
            src_ref=sb.at[at], dst_ref=rb.at[at], send_sem=rsend.at[at], recv_sem=rrecv.at[at],
            device_id=(r, right if i < 3 else left), device_id_type=MESH,
        )

    attend(opp)
    sb[0] = project(ho, ow, 0)
    rs(0, 0).start()
    sb[3] = project(ho, ow, 1)
    rs(0, 3).start()
    attend(right)
    sb[2] = project(ho, ow, 1)
    rs(0, 2).start()
    part = project(ho, ow, 0)
    rs(0, 0).wait_recv()
    sb[1] = (part.astype(F32) + rb[0].astype(F32)).astype(BF16)
    rs(0, 1).start()
    attend(left)
    sb[5] = project(ho, ow, 0)
    rs(0, 5).start()
    part = project(ho, ow, 1)
    rs(0, 3).wait_recv()
    sb[4] = (part.astype(F32) + rb[3].astype(F32)).astype(BF16)
    rs(0, 4).start()
    attend(y)
    for n in range(2):
        own[:, n * HALF:(n + 1) * HALF] = project(ho, ow, n)

    mine = pl.ds(pl.multiple_of(y * CH, CH), CH)
    for i in (1, 2, 4, 5):
        rs(0, i).wait_recv()

    def mix(i, carry):
        at = pl.multiple_of(i * 16, 16)
        rows = pl.ds(at, 16)
        x = tok[pl.ds(pl.multiple_of(y * CH + i * 16, 16), 16), :].astype(F32)
        o = own[rows, :].astype(F32)
        add_a = rb[1, rows, :].astype(F32) + rb[5, rows, :].astype(F32)
        add_b = rb[2, rows, :].astype(F32) + rb[4, rows, :].astype(F32)
        x = x + o + jnp.concatenate([add_a, add_b], axis=1)
        res[rows, :] = x
        ms = jnp.mean(x * x, axis=-1, keepdims=True)
        mid[pl.ds(pl.multiple_of(y * CH + i * 16, 16), 16), :] = (
            x * lax.rsqrt(ms + EPS) * g2_ref[...]
        ).astype(BF16)
        return carry

    lax.fori_loop(0, CH // 16, mix, 0)

    def ag(round_, i, buf):
        at = round_ * 6 + i
        chunk = (y, y, left, y, y, right)[i]
        half = (0, 1, 0, 1, 0, 1)[i]
        where = buf.at[pl.ds(pl.multiple_of(chunk * CH, CH), CH), pl.ds(half * HALF, HALF)]
        return pltpu.make_async_remote_copy(
            src_ref=where, dst_ref=where, send_sem=asend.at[at], recv_sem=arecv.at[at],
            device_id=(r, right if i < 3 else left), device_id_type=MESH,
        )

    def gather_start(round_, buf):
        for i in (0, 3, 1, 4):
            ag(round_, i, buf).start()

    def gather_pass(round_, buf):
        ag(round_, 0, buf).wait_recv()
        ag(round_, 2, buf).start()
        ag(round_, 3, buf).wait_recv()
        ag(round_, 5, buf).start()

    gather_start(0, mid)
    for c in loads[4:]:
        c.wait()

    def chunk_rows(chunk):
        return mid[pl.ds(pl.multiple_of(chunk * CH, CH), CH), :]

    def feed(x):
        hs = []
        for n in range(2):
            cols = slice(n * 256, (n + 1) * 256)
            g = jnp.dot(x, gw[:, cols], preferred_element_type=F32)
            u = jnp.dot(x, uw[:, cols], preferred_element_type=F32)
            hs.append((g / (1.0 + jnp.exp(-g)) * u).astype(BF16))
        return jnp.concatenate(hs, axis=1)

    h = feed(chunk_rows(y))
    for n in range(2):
        own2[:, n * HALF:(n + 1) * HALF] = project(h, dw, n)
    gather_pass(0, mid)
    ag(0, 1, mid).wait_recv()
    ag(0, 4, mid).wait_recv()
    h = feed(jnp.concatenate([chunk_rows(left), chunk_rows(right)], axis=0))
    part = project(h, dw, 0)
    sb[11] = part[:CH]
    rs(1, 5).start()
    sb[7] = part[CH:]
    part = project(h, dw, 1)
    sb[10] = part[:CH]
    sb[8] = part[CH:]
    rs(1, 2).start()
    ag(0, 2, mid).wait_recv()
    ag(0, 5, mid).wait_recv()
    h = feed(chunk_rows(opp))
    sb[6] = project(h, dw, 0)
    rs(1, 0).start()
    sb[9] = project(h, dw, 1)
    rs(1, 3).start()
    rs(1, 0).wait_recv()
    sb[7] = (sb[7].astype(F32) + rb[6].astype(F32)).astype(BF16)
    rs(1, 1).start()
    rs(1, 3).wait_recv()
    sb[10] = (sb[10].astype(F32) + rb[9].astype(F32)).astype(BF16)
    rs(1, 4).start()
    for i in (1, 2, 4, 5):
        rs(1, i).wait_recv()

    def finish(i, carry):
        rows = pl.ds(pl.multiple_of(i * 16, 16), 16)
        o = own2[rows, :].astype(F32)
        add_a = rb[7, rows, :].astype(F32) + rb[11, rows, :].astype(F32)
        add_b = rb[8, rows, :].astype(F32) + rb[10, rows, :].astype(F32)
        x = res[rows, :] + (o + jnp.concatenate([add_a, add_b], axis=1))
        outb[pl.ds(pl.multiple_of(y * CH + i * 16, 16), 16), :] = x.astype(BF16)
        return carry

    lax.fori_loop(0, CH // 16, finish, 0)
    gather_start(1, outb)

    def put(i, chunk):
        rows = pl.ds(pl.multiple_of(chunk * CH, CH), CH)
        return pltpu.make_async_copy(outb.at[rows, :], out_h.at[rows, :], oo.at[i])

    put(0, y).start()
    gather_pass(1, outb)
    ag(1, 1, outb).wait_recv()
    put(1, left).start()
    ag(1, 4, outb).wait_recv()
    put(2, right).start()
    ag(1, 2, outb).wait_recv()
    ag(1, 5, outb).wait_recv()
    put(3, opp).start()

    for k in range(1, 5):
        direct(k).wait_send()
        forward(k - 1, 0).wait_send()
    for i in range(6):
        rs(0, i).wait_send()
        rs(1, i).wait_send()
        ag(0, i, mid).wait_send()
        ag(1, i, outb).wait_send()
    kv_copy.wait()
    for i, chunk in enumerate((y, left, right, opp)):
        put(i, chunk).wait()


def body(tokens, segment_ids, mixer_gain, query_weight, pair_weight, output_weight, feed_gain,
         gate_weight, up_weight, down_weight):
    base, inner = rope_tables()
    hbm = pl.BlockSpec(memory_space=pl.ANY)
    vm = pl.BlockSpec(memory_space=pltpu.VMEM)
    dma = pltpu.SemaphoreType.DMA
    return pl.pallas_call(
        kernel,
        out_shape=(
            jax.ShapeDtypeStruct((T, D), BF16),
            jax.ShapeDtypeStruct((T, 128), BF16),
        ),
        in_specs=[hbm, vm, vm, vm, vm, vm] + [hbm] * 6,
        out_specs=(hbm, hbm),
        scratch_shapes=[
            pltpu.VMEM((T, D), BF16),
            pltpu.VMEM((T, D), BF16),
            pltpu.VMEM((D, 128), BF16),
            pltpu.VMEM((D, C), BF16),
            pltpu.VMEM((C, D), BF16),
            pltpu.VMEM((D, F), BF16),
            pltpu.VMEM((D, F), BF16),
            pltpu.VMEM((F, D), BF16),
            pltpu.VMEM((BLOCKS + 1, KROWS, 128), BF16),
            pltpu.VMEM((BLOCKS + 1, 128, T), BF16),
            pltpu.VMEM(((BLOCKS + 1) * T, 128), BF16),
            pltpu.VMEM((HEADS, T, 128), BF16),
            pltpu.VMEM((HEADS, T, BLOCKS * T), F32),
            pltpu.VMEM((HEADS, T, 128), F32),
            pltpu.VMEM((HEADS * CH, (BLOCKS + 1) * T), BF16),
            pltpu.VMEM((CH, C), BF16),
            pltpu.VMEM((12, CH, HALF), BF16),
            pltpu.VMEM((12, CH, HALF), BF16),
            pltpu.VMEM((CH, D), BF16),
            pltpu.VMEM((CH, D), BF16),
            pltpu.VMEM((CH, D), F32),
            pltpu.VMEM((T, D), BF16),
            pltpu.VMEM((T, D), BF16),
            dma((7,)), dma, dma((4,)),
            dma((4,)), dma((4,)), dma((4,)), dma((4,)),
            dma((12,)), dma((12,)), dma((12,)), dma((12,)),
        ],
        compiler_params=pltpu.CompilerParams(
            collective_id=0, has_side_effects=True, vmem_limit_bytes=64 * 1024 * 1024 - 65536
        ),
        name="block",
    )(
        tokens, segment_ids.reshape(1, T), mixer_gain.reshape(1, D), feed_gain.reshape(1, D),
        jnp.asarray(base), jnp.asarray(inner),
        query_weight, pair_weight, output_weight, gate_weight, up_weight, down_weight,
    )


def solution(mesh):
    return jax.shard_map(
        body,
        mesh=mesh,
        in_specs=(
            P("req", None),
            P("req"),
            P(),
            P(None, "tp"),
            P(None, "tp"),
            P("tp", None),
            P(),
            P(None, "tp"),
            P(None, "tp"),
            P("tp", None),
        ),
        out_specs=(P("req", None), P("req", "tp")),
        check_vma=False,
    )
```

```python
import math

import jax
import jax.numpy as jnp
import numpy as np
from jax import lax
from jax.experimental import pallas as pl
from jax.experimental.pallas import tpu as pltpu
from jax.sharding import PartitionSpec as P

MESH = pl.DeviceIdType.MESH
F32 = jnp.float32
BF16 = jnp.bfloat16
NEG = -1e30
EPS = 1e-05

T = 256
D = 2048
REQ = 64
TP = 4
HEADS = 8
HD = 64
C = 512
F = 512
CH = T // TP
HALF = D // 2
BLOCKS = 8
KROWS = T + 16


def rope_tables():
    freq = np.exp(-math.log(10000.0) * np.arange(32, dtype=np.float32) / np.float32(32)).astype(np.float32)
    freq = np.tile(freq.astype(np.float64), 4)[None, :]
    base = (np.arange(REQ) * T)[:, None] * freq
    inner = np.arange(T)[:, None] * freq
    base = np.stack([np.cos(base), np.sin(base)]).astype(np.float32)
    inner = np.stack([np.cos(inner), np.sin(inner)]).astype(np.float32)
    return base, inner


def iota(shape, dim):
    return lax.broadcasted_iota(jnp.int32, shape, dim)


def kernel(
    tok_h, seg_ref, g1_ref, g2_ref, base_ref, inner_ref,
    qw_h, pw_h, ow_h, gw_h, uw_h, dw_h,
    out_h, kvout_h,
    tok, normed, pw, qw, ow, gw, uw, dw,
    kvb, kT, vx, qa, S, M, Pm, ho, sb, rb, own, own2, res, mid, outb,
    ld, kvo, oo, dsend, drecv, fsend, frecv, rsend, rrecv, asend, arecv,
):
    r = lax.axis_index("req")
    y = lax.axis_index("tp")
    core = lax.rem(r, 2)
    partner = r + 1 - 2 * core
    right = lax.rem(y + 1, TP)
    left = lax.rem(y + 3, TP)
    opp = lax.rem(y + 2, TP)

    barrier = pltpu.get_barrier_semaphore()
    for k in range(1, 5):
        @pl.when(r >= 2 * k)
        def _():
            pl.semaphore_signal(barrier, inc=1, device_id=(r - 2 * k, y), device_id_type=MESH)

    pl.semaphore_signal(barrier, inc=1, device_id=(partner, y), device_id_type=MESH)
    pl.semaphore_signal(barrier, inc=1, device_id=(r, right), device_id_type=MESH)
    pl.semaphore_signal(barrier, inc=1, device_id=(r, left), device_id_type=MESH)

    def load(i, src, dst):
        return pltpu.make_async_copy(src, dst, ld.at[i])

    loads = [
        load(i, s, d)
        for i, (s, d) in enumerate(
            [(tok_h, tok), (pw_h, pw), (qw_h, qw), (ow_h, ow), (gw_h, gw), (uw_h, uw), (dw_h, dw)]
        )
    ]
    for c in loads:
        c.start()

    ca, sa = base_ref[0, pl.ds(r, 1), :], base_ref[1, pl.ds(r, 1), :]
    cb, sn = inner_ref[0], inner_ref[1]
    cos = ca * cb - sa * sn
    sin = sa * cb + ca * sn
    lane = iota((T, 128), 1)
    first = lax.rem(lane, 64) < 32
    s_up = jnp.where(first, -sin, 0.0)
    s_dn = jnp.where(first, 0.0, sin)

    def rotate(x, c, su, sd):
        return x * c + pltpu.roll(x, 96, 1) * su + pltpu.roll(x, 32, 1) * sd

    seg_row = seg_ref[...].astype(F32)
    seg_col = jnp.broadcast_to(seg_row, (128, T)).T
    loads[0].wait()

    def norm_rows(i, carry):
        rows = pl.ds(pl.multiple_of(i * 16, 16), 16)
        x = tok[rows, :].astype(F32)
        ms = jnp.mean(x * x, axis=-1, keepdims=True)
        normed[rows, :] = (x * lax.rsqrt(ms + EPS) * g1_ref[...]).astype(BF16)
        return carry

    lax.fori_loop(0, T // 16, norm_rows, 0, unroll=2)

    loads[1].wait()
    kv = jnp.dot(normed[...], pw[...], preferred_element_type=F32)
    isk = lane < 64
    kv = rotate(kv, jnp.where(isk, cos, 1.0), jnp.where(isk, s_up, 0.0), jnp.where(isk, s_dn, 0.0))
    kvb[0, 0:T, :] = kv.astype(BF16)
    srow = iota((16, 128), 0)
    kvb[0, T:KROWS, :] = jnp.where(
        srow == 0, seg_row[:, :128], jnp.where(srow == 1, seg_row[:, 128:], 0.0)
    ).astype(BF16)

    pl.semaphore_wait(barrier, 3 + jnp.minimum(4, (REQ - 1 - r) // 2))

    def direct(k):
        return pltpu.make_async_remote_copy(
            src_ref=kvb.at[0], dst_ref=kvb.at[2 * k],
            send_sem=dsend.at[k - 1], recv_sem=drecv.at[k - 1],
            device_id=(r + 2 * k, y), device_id_type=MESH,
        )

    def forward(j, src):
        return pltpu.make_async_remote_copy(
            src_ref=kvb.at[src], dst_ref=kvb.at[2 * j + 1],
            send_sem=fsend.at[j], recv_sem=frecv.at[j],
            device_id=(partner, y), device_id_type=MESH,
        )

    for k in range(1, 5):
        @pl.when(r + 2 * k < REQ)
        def _():
            direct(k).start()

    for d in range(1, BLOCKS + 1):
        @pl.when(r < d)
        def _():
            kvb[d] = jnp.zeros((KROWS, 128), BF16)


    @pl.when(core == 0)
    def _():
        forward(0, 0).start()

    kv_copy = pltpu.make_async_copy(kvb.at[0, 0:T, :], kvout_h, kvo)
    kv_copy.start()

    loads[2].wait()
    qpen = jnp.where((lane - 64).astype(F32) == seg_col, NEG, 0.0)
    qpen = jnp.where(lane < 80, qpen, 0.0)
    for n in range(2):
        q4 = jnp.dot(normed[...], qw[:, n * 256:(n + 1) * 256], preferred_element_type=F32)
        for i in range(2):
            q2 = rotate(q4[:, i * 128:(i + 1) * 128], cos, s_up, s_dn) * (HD ** -0.5)
            h = n * 4 + i * 2
            qa[h] = jnp.where(isk, q2, qpen).astype(BF16)
            qa[h + 1] = jnp.where(isk, pltpu.roll(q2, 64, 1), qpen).astype(BF16)

    def prepare(d):
        kv = kvb[d, 0:T, :].astype(F32)
        ids = kvb[d, T:KROWS, :].astype(F32)
        ids = jnp.concatenate([ids[0:1], ids[1:2]], axis=1) + jnp.where(r >= d, 0.0, 100.0)
        row = iota((128, T), 0)
        differs = jnp.where((row - 64).astype(F32) == ids, 0.0, 1.0)
        kT[d] = jnp.where(row < 64, kv.T, jnp.where(row < 80, differs, 0.0)).astype(BF16)
        vx[d * T:(d + 1) * T, :] = jnp.where(isk, pltpu.roll(kv, 64, 1), 1.0).astype(BF16)

    def top(d):
        prepare(d)

        def body(h, carry):
            s = jnp.dot(qa[h], kT[d], preferred_element_type=F32)
            at = (d % BLOCKS) * T
            if d in (0, BLOCKS):
                seen = iota((T, T), 1) <= iota((T, T), 0)
                s = jnp.where(seen, s if d == 0 else S[h, :, 0:T], NEG if d == 0 else s)
            S[h, :, at:at + T] = s
            top = jnp.maximum(s[:, :128], s[:, 128:])
            M[h] = top if d == 0 else jnp.maximum(M[h], top)
            return carry

        lax.fori_loop(0, HEADS, body, 0)

    def arrive(k):
        @pl.when(r >= 2 * k)
        def _():
            direct(k).wait_recv()

        @pl.when((r >= 2 * k) & (core == 1))
        def _():
            forward(k - 1, 2 * k).start()

        if k < 4:
            @pl.when((r >= 2 * k) & (core == 0))
            def _():
                forward(k, 2 * k).start()

    def handed(j):
        @pl.when(r >= 2 * j + 1)
        def _():
            forward(j, 0).wait_recv()

    top(0)
    arrive(1)
    top(2)
    for k in range(2, 5):
        arrive(k)
        handed(k - 2)
        top(2 * k - 3)
        top(2 * k)
    handed(3)
    top(7)

    loads[3].wait()

    def attend(chunk):
        r0 = pl.multiple_of(chunk * CH, CH)
        rows = pl.ds(r0, CH)

        def head(h, carry):
            m = jnp.max(M[h, rows, :], axis=1, keepdims=True)
            to = pl.ds(pl.multiple_of(h * CH, CH), CH)
            for b in range(BLOCKS):
                p = jnp.exp(S[h, rows, b * T:(b + 1) * T] - m)
                if b == 0:
                    seen = iota((CH, T), 1) <= iota((CH, T), 0) + r0
                    Pm[to, BLOCKS * T:(BLOCKS + 1) * T] = jnp.where(seen, 0.0, p).astype(BF16)
                    p = jnp.where(seen, p, 0.0)
                Pm[to, b * T:(b + 1) * T] = p.astype(BF16)
            return carry

        lax.fori_loop(0, HEADS, head, 0)
        low = iota((CH, 128), 1) < 64
        for n in range(2):
            o = jnp.dot(Pm[n * 256:(n + 1) * 256, :], vx[...], preferred_element_type=F32)
            o = o / pltpu.roll(o, 64, 1)
            for i in range(2):
                even, odd = o[i * 128:i * 128 + 64], o[i * 128 + 64:i * 128 + 128]
                at = (n * 2 + i) * 128
                ho[:, at:at + 128] = jnp.where(low, even, pltpu.roll(odd, 64, 1)).astype(BF16)

    def project(x, w, n):
        return jnp.dot(x[...], w[:, n * HALF:(n + 1) * HALF], preferred_element_type=F32).astype(BF16)

    def rs(round_, i):
        at = round_ * 6 + i
        return pltpu.make_async_remote_copy(
            src_ref=sb.at[at], dst_ref=rb.at[at], send_sem=rsend.at[at], recv_sem=rrecv.at[at],
            device_id=(r, right if i < 3 else left), device_id_type=MESH,
        )

    attend(opp)
    sb[0] = project(ho, ow, 0)
    rs(0, 0).start()
    sb[3] = project(ho, ow, 1)
    rs(0, 3).start()
    attend(right)
    sb[2] = project(ho, ow, 1)
    rs(0, 2).start()
    part = project(ho, ow, 0)
    rs(0, 0).wait_recv()
    sb[1] = (part.astype(F32) + rb[0].astype(F32)).astype(BF16)
    rs(0, 1).start()
    attend(left)
    sb[5] = project(ho, ow, 0)
    rs(0, 5).start()
    part = project(ho, ow, 1)
    rs(0, 3).wait_recv()
    sb[4] = (part.astype(F32) + rb[3].astype(F32)).astype(BF16)
    rs(0, 4).start()
    attend(y)
    for n in range(2):
        own[:, n * HALF:(n + 1) * HALF] = project(ho, ow, n)

    mine = pl.ds(pl.multiple_of(y * CH, CH), CH)
    for i in (1, 2, 4, 5):
        rs(0, i).wait_recv()

    def mix(i, carry):
        at = pl.multiple_of(i * 16, 16)
        rows = pl.ds(at, 16)
        x = tok[pl.ds(pl.multiple_of(y * CH + i * 16, 16), 16), :].astype(F32)
        o = own[rows, :].astype(F32)
        add_a = rb[1, rows, :].astype(F32) + rb[5, rows, :].astype(F32)
        add_b = rb[2, rows, :].astype(F32) + rb[4, rows, :].astype(F32)
        x = x + o + jnp.concatenate([add_a, add_b], axis=1)
        res[rows, :] = x
        ms = jnp.mean(x * x, axis=-1, keepdims=True)
        mid[pl.ds(pl.multiple_of(y * CH + i * 16, 16), 16), :] = (
            x * lax.rsqrt(ms + EPS) * g2_ref[...]
        ).astype(BF16)
        return carry

    lax.fori_loop(0, CH // 16, mix, 0)

    def ag(round_, i, buf):
        at = round_ * 6 + i
        chunk = (y, y, left, y, y, right)[i]
        half = (0, 1, 0, 1, 0, 1)[i]
        where = buf.at[pl.ds(pl.multiple_of(chunk * CH, CH), CH), pl.ds(half * HALF, HALF)]
        return pltpu.make_async_remote_copy(
            src_ref=where, dst_ref=where, send_sem=asend.at[at], recv_sem=arecv.at[at],
            device_id=(r, right if i < 3 else left), device_id_type=MESH,
        )

    def gather_start(round_, buf):
        for i in (0, 3, 1, 4):
            ag(round_, i, buf).start()

    def gather_pass(round_, buf):
        ag(round_, 0, buf).wait_recv()
        ag(round_, 2, buf).start()
        ag(round_, 3, buf).wait_recv()
        ag(round_, 5, buf).start()

    gather_start(0, mid)
    for c in loads[4:]:
        c.wait()

    def chunk_rows(chunk):
        return mid[pl.ds(pl.multiple_of(chunk * CH, CH), CH), :]

    def feed(x):
        hs = []
        for n in range(2):
            cols = slice(n * 256, (n + 1) * 256)
            g = jnp.dot(x, gw[:, cols], preferred_element_type=F32)
            u = jnp.dot(x, uw[:, cols], preferred_element_type=F32)
            hs.append((g / (1.0 + jnp.exp(-g)) * u).astype(BF16))
        return jnp.concatenate(hs, axis=1)

    h = feed(chunk_rows(y))
    for n in range(2):
        own2[:, n * HALF:(n + 1) * HALF] = project(h, dw, n)
    gather_pass(0, mid)
    ag(0, 1, mid).wait_recv()
    ag(0, 4, mid).wait_recv()
    h = feed(jnp.concatenate([chunk_rows(left), chunk_rows(right)], axis=0))
    part = project(h, dw, 0)
    sb[11] = part[:CH]
    rs(1, 5).start()
    sb[7] = part[CH:]
    part = project(h, dw, 1)
    sb[10] = part[:CH]
    sb[8] = part[CH:]
    rs(1, 2).start()
    ag(0, 2, mid).wait_recv()
    ag(0, 5, mid).wait_recv()
    h = feed(chunk_rows(opp))
    sb[6] = project(h, dw, 0)
    rs(1, 0).start()
    sb[9] = project(h, dw, 1)
    rs(1, 3).start()
    rs(1, 0).wait_recv()
    sb[7] = (sb[7].astype(F32) + rb[6].astype(F32)).astype(BF16)
    rs(1, 1).start()
    rs(1, 3).wait_recv()
    sb[10] = (sb[10].astype(F32) + rb[9].astype(F32)).astype(BF16)
    rs(1, 4).start()
    for i in (1, 2, 4, 5):
        rs(1, i).wait_recv()

    def finish(i, carry):
        rows = pl.ds(pl.multiple_of(i * 16, 16), 16)
        o = own2[rows, :].astype(F32)
        add_a = rb[7, rows, :].astype(F32) + rb[11, rows, :].astype(F32)
        add_b = rb[8, rows, :].astype(F32) + rb[10, rows, :].astype(F32)
        x = res[rows, :] + (o + jnp.concatenate([add_a, add_b], axis=1))
        outb[pl.ds(pl.multiple_of(y * CH + i * 16, 16), 16), :] = x.astype(BF16)
        return carry

    lax.fori_loop(0, CH // 16, finish, 0)
    gather_start(1, outb)

    def put(i, chunk):
        rows = pl.ds(pl.multiple_of(chunk * CH, CH), CH)
        return pltpu.make_async_copy(outb.at[rows, :], out_h.at[rows, :], oo.at[i])

    put(0, y).start()
    gather_pass(1, outb)
    ag(1, 1, outb).wait_recv()
    put(1, left).start()
    ag(1, 4, outb).wait_recv()
    put(2, right).start()
    ag(1, 2, outb).wait_recv()
    ag(1, 5, outb).wait_recv()
    put(3, opp).start()

    for k in range(1, 5):
        @pl.when(r + 2 * k < REQ)
        def _():
            direct(k).wait_send()

        @pl.when(r >= 2 * (k - 1) + 2 * core)
        def _():
            forward(k - 1, 0).wait_send()

    for i in range(6):
        rs(0, i).wait_send()
        rs(1, i).wait_send()
        ag(0, i, mid).wait_send()
        ag(1, i, outb).wait_send()
    kv_copy.wait()
    for i, chunk in enumerate((y, left, right, opp)):
        put(i, chunk).wait()


def body(tokens, segment_ids, mixer_gain, query_weight, pair_weight, output_weight, feed_gain,
         gate_weight, up_weight, down_weight):
    base, inner = rope_tables()
    hbm = pl.BlockSpec(memory_space=pl.ANY)
    vm = pl.BlockSpec(memory_space=pltpu.VMEM)
    dma = pltpu.SemaphoreType.DMA
    return pl.pallas_call(
        kernel,
        out_shape=(
            jax.ShapeDtypeStruct((T, D), BF16),
            jax.ShapeDtypeStruct((T, 128), BF16),
        ),
        in_specs=[hbm, vm, vm, vm, vm, vm] + [hbm] * 6,
        out_specs=(hbm, hbm),
        scratch_shapes=[
            pltpu.VMEM((T, D), BF16),
            pltpu.VMEM((T, D), BF16),
            pltpu.VMEM((D, 128), BF16),
            pltpu.VMEM((D, C), BF16),
            pltpu.VMEM((C, D), BF16),
            pltpu.VMEM((D, F), BF16),
            pltpu.VMEM((D, F), BF16),
            pltpu.VMEM((F, D), BF16),
            pltpu.VMEM((BLOCKS + 1, KROWS, 128), BF16),
            pltpu.VMEM((BLOCKS + 1, 128, T), BF16),
            pltpu.VMEM(((BLOCKS + 1) * T, 128), BF16),
            pltpu.VMEM((HEADS, T, 128), BF16),
            pltpu.VMEM((HEADS, T, BLOCKS * T), F32),
            pltpu.VMEM((HEADS, T, 128), F32),
            pltpu.VMEM((HEADS * CH, (BLOCKS + 1) * T), BF16),
            pltpu.VMEM((CH, C), BF16),
            pltpu.VMEM((12, CH, HALF), BF16),
            pltpu.VMEM((12, CH, HALF), BF16),
            pltpu.VMEM((CH, D), BF16),
            pltpu.VMEM((CH, D), BF16),
            pltpu.VMEM((CH, D), F32),
            pltpu.VMEM((T, D), BF16),
            pltpu.VMEM((T, D), BF16),
            dma((7,)), dma, dma((4,)),
            dma((4,)), dma((4,)), dma((4,)), dma((4,)),
            dma((12,)), dma((12,)), dma((12,)), dma((12,)),
        ],
        compiler_params=pltpu.CompilerParams(
            collective_id=0, has_side_effects=True, vmem_limit_bytes=64 * 1024 * 1024 - 65536
        ),
        name="block",
    )(
        tokens, segment_ids.reshape(1, T), mixer_gain.reshape(1, D), feed_gain.reshape(1, D),
        jnp.asarray(base), jnp.asarray(inner),
        query_weight, pair_weight, output_weight, gate_weight, up_weight, down_weight,
    )


def solution(mesh):
    return jax.shard_map(
        body,
        mesh=mesh,
        in_specs=(
            P("req", None),
            P("req"),
            P(),
            P(None, "tp"),
            P(None, "tp"),
            P("tp", None),
            P(),
            P(None, "tp"),
            P(None, "tp"),
            P("tp", None),
        ),
        out_specs=(P("req", None), P("req", "tp")),
        check_vma=False,
    )
```

```python
import math

import jax
import jax.numpy as jnp
import numpy as np
from jax import lax
from jax.experimental import pallas as pl
from jax.experimental.pallas import tpu as pltpu
from jax.sharding import PartitionSpec as P

MESH = pl.DeviceIdType.MESH
F32 = jnp.float32
BF16 = jnp.bfloat16
NEG = -1e30
EPS = 1e-05

T = 256
D = 2048
REQ = 64
TP = 4
HEADS = 8
HD = 64
C = 512
F = 512
CH = T // TP
HALF = D // 2
BLOCKS = 8
KROWS = T + 16


def rope_tables():
    freq = np.exp(-math.log(10000.0) * np.arange(32, dtype=np.float32) / np.float32(32)).astype(np.float32)
    freq = np.tile(freq.astype(np.float64), 4)[None, :]
    base = (np.arange(REQ) * T)[:, None] * freq
    inner = np.arange(T)[:, None] * freq
    base = np.stack([np.cos(base), np.sin(base)]).astype(np.float32)
    inner = np.stack([np.cos(inner), np.sin(inner)]).astype(np.float32)
    return base, inner


def iota(shape, dim):
    return lax.broadcasted_iota(jnp.int32, shape, dim)


def kernel(
    tok_h, seg_ref, g1_ref, g2_ref, base_ref, inner_ref,
    qw_h, pw_h, ow_h, gw_h, uw_h, dw_h,
    out_h, kvout_h,
    tok, normed, pw, qw, ow, gw, uw, dw,
    kvb, kT, vx, qa, S, M, Pm, ho, sb, rb, own, own2, res, mid, outb,
    ld, kvo, oo, dsend, drecv, fsend, frecv, rsend, rrecv, asend, arecv,
):
    r = lax.axis_index("req")
    y = lax.axis_index("tp")
    core = lax.rem(r, 2)
    partner = r + 1 - 2 * core
    right = lax.rem(y + 1, TP)
    left = lax.rem(y + 3, TP)
    opp = lax.rem(y + 2, TP)

    barrier = pltpu.get_barrier_semaphore()
    for k in range(1, 5):
        @pl.when(r >= 2 * k)
        def _():
            pl.semaphore_signal(barrier, inc=1, device_id=(r - 2 * k, y), device_id_type=MESH)

    pl.semaphore_signal(barrier, inc=1, device_id=(partner, y), device_id_type=MESH)
    pl.semaphore_signal(barrier, inc=1, device_id=(r, right), device_id_type=MESH)
    pl.semaphore_signal(barrier, inc=1, device_id=(r, left), device_id_type=MESH)

    def load(i, src, dst):
        return pltpu.make_async_copy(src, dst, ld.at[i])

    loads = [
        load(i, s, d)
        for i, (s, d) in enumerate(
            [(tok_h, tok), (pw_h, pw), (qw_h, qw), (ow_h, ow), (gw_h, gw), (uw_h, uw), (dw_h, dw)]
        )
    ]
    for c in loads:
        c.start()

    ca, sa = base_ref[0, pl.ds(r, 1), :], base_ref[1, pl.ds(r, 1), :]
    cb, sn = inner_ref[0], inner_ref[1]
    cos = ca * cb - sa * sn
    sin = sa * cb + ca * sn
    lane = iota((T, 128), 1)
    first = lax.rem(lane, 64) < 32
    s_up = jnp.where(first, -sin, 0.0)
    s_dn = jnp.where(first, 0.0, sin)

    def rotate(x, c, su, sd):
        return x * c + pltpu.roll(x, 96, 1) * su + pltpu.roll(x, 32, 1) * sd

    seg_row = seg_ref[...].astype(F32)
    seg_col = jnp.broadcast_to(seg_row, (128, T)).T
    loads[0].wait()

    def norm_rows(i, carry):
        rows = pl.ds(pl.multiple_of(i * 16, 16), 16)
        x = tok[rows, :].astype(F32)
        ms = jnp.mean(x * x, axis=-1, keepdims=True)
        normed[rows, :] = (x * lax.rsqrt(ms + EPS) * g1_ref[...]).astype(BF16)
        return carry

    lax.fori_loop(0, T // 16, norm_rows, 0, unroll=2)

    loads[1].wait()
    kv = jnp.dot(normed[...], pw[...], preferred_element_type=F32)
    isk = lane < 64
    kv = rotate(kv, jnp.where(isk, cos, 1.0), jnp.where(isk, s_up, 0.0), jnp.where(isk, s_dn, 0.0))
    kvb[0, 0:T, :] = kv.astype(BF16)
    srow = iota((16, 128), 0)
    kvb[0, T:KROWS, :] = jnp.where(
        srow == 0, seg_row[:, :128], jnp.where(srow == 1, seg_row[:, 128:], 0.0)
    ).astype(BF16)

    pl.semaphore_wait(barrier, 3 + jnp.minimum(4, (REQ - 1 - r) // 2))

    def direct(k):
        return pltpu.make_async_remote_copy(
            src_ref=kvb.at[0], dst_ref=kvb.at[2 * k],
            send_sem=dsend.at[k - 1], recv_sem=drecv.at[k - 1],
            device_id=(r + 2 * k, y), device_id_type=MESH,
        )

    def forward(j, src):
        return pltpu.make_async_remote_copy(
            src_ref=kvb.at[src], dst_ref=kvb.at[2 * j + 1],
            send_sem=fsend.at[j], recv_sem=frecv.at[j],
            device_id=(partner, y), device_id_type=MESH,
        )

    for k in range(1, 5):
        @pl.when(r + 2 * k < REQ)
        def _():
            direct(k).start()

    for d in range(1, BLOCKS + 1):
        @pl.when(r < d)
        def _():
            kvb[d] = jnp.zeros((KROWS, 128), BF16)


    @pl.when(core == 0)
    def _():
        forward(0, 0).start()

    kv_copy = pltpu.make_async_copy(kvb.at[0, 0:T, :], kvout_h, kvo)
    kv_copy.start()

    loads[2].wait()
    qpen = jnp.where((lane - 64).astype(F32) == seg_col, NEG, 0.0)
    qpen = jnp.where(lane < 80, qpen, 0.0)
    for n in range(2):
        q4 = jnp.dot(normed[...], qw[:, n * 256:(n + 1) * 256], preferred_element_type=F32)
        for i in range(2):
            q2 = rotate(q4[:, i * 128:(i + 1) * 128], cos, s_up, s_dn) * (HD ** -0.5)
            h = n * 4 + i * 2
            qa[h] = jnp.where(isk, q2, qpen).astype(BF16)
            qa[h + 1] = jnp.where(isk, pltpu.roll(q2, 64, 1), qpen).astype(BF16)

    def prepare(d):
        kv = kvb[d, 0:T, :].astype(F32)
        ids = kvb[d, T:KROWS, :].astype(F32)
        ids = jnp.concatenate([ids[0:1], ids[1:2]], axis=1) + jnp.where(r >= d, 0.0, 100.0)
        row = iota((128, T), 0)
        differs = jnp.where((row - 64).astype(F32) == ids, 0.0, 1.0)
        kT[d] = jnp.where(row < 64, kv.T, jnp.where(row < 80, differs, 0.0)).astype(BF16)
        v1 = jnp.where(isk, pltpu.roll(kv, 64, 1), 1.0).astype(BF16)
        vx[d * T:(d + 1) * T, :128] = v1
        vx[d * T:(d + 1) * T, 128:] = v1

    def top(*ds):
        for d in ds:
            prepare(d)

        def body(h, carry):
            best = None if 0 in ds else M[h]
            for d in ds:
                s = jnp.dot(qa[h], kT[d], preferred_element_type=F32)
                at = (d % BLOCKS) * T
                if d in (0, BLOCKS):
                    seen = iota((T, T), 1) <= iota((T, T), 0)
                    s = jnp.where(seen, s if d == 0 else S[h, :, 0:T], NEG if d == 0 else s)
                S[h, :, at:at + T] = s
                m = jnp.maximum(s[:, :128], s[:, 128:])
                best = m if best is None else jnp.maximum(best, m)
            M[h] = best
            return carry

        lax.fori_loop(0, HEADS, body, 0)

    def arrive(k):
        @pl.when(r >= 2 * k)
        def _():
            direct(k).wait_recv()

        @pl.when((r >= 2 * k) & (core == 1))
        def _():
            forward(k - 1, 2 * k).start()

        if k < 4:
            @pl.when((r >= 2 * k) & (core == 0))
            def _():
                forward(k, 2 * k).start()

    def handed(j):
        @pl.when(r >= 2 * j + 1)
        def _():
            forward(j, 0).wait_recv()

    top(0)
    arrive(1)
    top(2)
    for k in range(2, 5):
        arrive(k)
        handed(k - 2)
        top(2 * k - 3, 2 * k)
    handed(3)
    top(7)

    loads[3].wait()

    def attend(chunk):
        r0 = pl.multiple_of(chunk * CH, CH)
        rows = pl.ds(r0, CH)

        def head(h, carry):
            m = jnp.max(M[h, rows, :], axis=1, keepdims=True)
            to = pl.ds(pl.multiple_of(h * CH, CH), CH)
            for b in range(BLOCKS):
                p = jnp.exp(S[h, rows, b * T:(b + 1) * T] - m)
                if b == 0:
                    seen = iota((CH, T), 1) <= iota((CH, T), 0) + r0
                    Pm[to, BLOCKS * T:(BLOCKS + 1) * T] = jnp.where(seen, 0.0, p).astype(BF16)
                    p = jnp.where(seen, p, 0.0)
                Pm[to, b * T:(b + 1) * T] = p.astype(BF16)
            return carry

        lax.fori_loop(0, HEADS, head, 0)
        low = iota((CH, 128), 1) < 64
        for n in range(2):
            o = jnp.dot(Pm[n * 256:(n + 1) * 256, :], vx[...], preferred_element_type=F32)
            o = o[:, :128]
            o = o / pltpu.roll(o, 64, 1)
            for i in range(2):
                even, odd = o[i * 128:i * 128 + 64], o[i * 128 + 64:i * 128 + 128]
                at = (n * 2 + i) * 128
                ho[:, at:at + 128] = jnp.where(low, even, pltpu.roll(odd, 64, 1)).astype(BF16)

    def project(x, w, n):
        return jnp.dot(x[...], w[:, n * HALF:(n + 1) * HALF], preferred_element_type=F32).astype(BF16)

    def rs(round_, i):
        at = round_ * 6 + i
        return pltpu.make_async_remote_copy(
            src_ref=sb.at[at], dst_ref=rb.at[at], send_sem=rsend.at[at], recv_sem=rrecv.at[at],
            device_id=(r, right if i < 3 else left), device_id_type=MESH,
        )

    attend(opp)
    sb[0] = project(ho, ow, 0)
    rs(0, 0).start()
    sb[3] = project(ho, ow, 1)
    rs(0, 3).start()
    attend(right)
    sb[2] = project(ho, ow, 1)
    rs(0, 2).start()
    part = project(ho, ow, 0)
    rs(0, 0).wait_recv()
    sb[1] = (part.astype(F32) + rb[0].astype(F32)).astype(BF16)
    rs(0, 1).start()
    attend(left)
    sb[5] = project(ho, ow, 0)
    rs(0, 5).start()
    part = project(ho, ow, 1)
    rs(0, 3).wait_recv()
    sb[4] = (part.astype(F32) + rb[3].astype(F32)).astype(BF16)
    rs(0, 4).start()
    attend(y)
    for n in range(2):
        own[:, n * HALF:(n + 1) * HALF] = project(ho, ow, n)

    mine = pl.ds(pl.multiple_of(y * CH, CH), CH)
    for i in (1, 2, 4, 5):
        rs(0, i).wait_recv()

    def mix(i, carry):
        at = pl.multiple_of(i * 16, 16)
        rows = pl.ds(at, 16)
        x = tok[pl.ds(pl.multiple_of(y * CH + i * 16, 16), 16), :].astype(F32)
        o = own[rows, :].astype(F32)
        add_a = rb[1, rows, :].astype(F32) + rb[5, rows, :].astype(F32)
        add_b = rb[2, rows, :].astype(F32) + rb[4, rows, :].astype(F32)
        x = x + o + jnp.concatenate([add_a, add_b], axis=1)
        res[rows, :] = x
        ms = jnp.mean(x * x, axis=-1, keepdims=True)
        mid[pl.ds(pl.multiple_of(y * CH + i * 16, 16), 16), :] = (
            x * lax.rsqrt(ms + EPS) * g2_ref[...]
        ).astype(BF16)
        return carry

    lax.fori_loop(0, CH // 16, mix, 0)

    def ag(round_, i, buf):
        at = round_ * 6 + i
        chunk = (y, y, left, y, y, right)[i]
        half = (0, 1, 0, 1, 0, 1)[i]
        where = buf.at[pl.ds(pl.multiple_of(chunk * CH, CH), CH), pl.ds(half * HALF, HALF)]
        return pltpu.make_async_remote_copy(
            src_ref=where, dst_ref=where, send_sem=asend.at[at], recv_sem=arecv.at[at],
            device_id=(r, right if i < 3 else left), device_id_type=MESH,
        )

    def gather_start(round_, buf):
        for i in (0, 3, 1, 4):
            ag(round_, i, buf).start()

    def gather_pass(round_, buf):
        ag(round_, 0, buf).wait_recv()
        ag(round_, 2, buf).start()
        ag(round_, 3, buf).wait_recv()
        ag(round_, 5, buf).start()

    gather_start(0, mid)
    for c in loads[4:]:
        c.wait()

    def chunk_rows(chunk):
        return mid[pl.ds(pl.multiple_of(chunk * CH, CH), CH), :]

    def feed(x):
        hs = []
        for n in range(2):
            cols = slice(n * 256, (n + 1) * 256)
            g = jnp.dot(x, gw[:, cols], preferred_element_type=F32)
            u = jnp.dot(x, uw[:, cols], preferred_element_type=F32)
            hs.append((g / (1.0 + jnp.exp(-g)) * u).astype(BF16))
        return jnp.concatenate(hs, axis=1)

    h = feed(chunk_rows(y))
    for n in range(2):
        own2[:, n * HALF:(n + 1) * HALF] = project(h, dw, n)
    gather_pass(0, mid)
    ag(0, 1, mid).wait_recv()
    ag(0, 4, mid).wait_recv()
    h = feed(jnp.concatenate([chunk_rows(left), chunk_rows(right)], axis=0))
    part = project(h, dw, 0)
    sb[11] = part[:CH]
    rs(1, 5).start()
    sb[7] = part[CH:]
    part = project(h, dw, 1)
    sb[10] = part[:CH]
    sb[8] = part[CH:]
    rs(1, 2).start()
    ag(0, 2, mid).wait_recv()
    ag(0, 5, mid).wait_recv()
    h = feed(chunk_rows(opp))
    sb[6] = project(h, dw, 0)
    rs(1, 0).start()
    sb[9] = project(h, dw, 1)
    rs(1, 3).start()
    rs(1, 0).wait_recv()
    sb[7] = (sb[7].astype(F32) + rb[6].astype(F32)).astype(BF16)
    rs(1, 1).start()
    rs(1, 3).wait_recv()
    sb[10] = (sb[10].astype(F32) + rb[9].astype(F32)).astype(BF16)
    rs(1, 4).start()
    for i in (1, 2, 4, 5):
        rs(1, i).wait_recv()

    def finish(i, carry):
        rows = pl.ds(pl.multiple_of(i * 16, 16), 16)
        o = own2[rows, :].astype(F32)
        add_a = rb[7, rows, :].astype(F32) + rb[11, rows, :].astype(F32)
        add_b = rb[8, rows, :].astype(F32) + rb[10, rows, :].astype(F32)
        x = res[rows, :] + (o + jnp.concatenate([add_a, add_b], axis=1))
        outb[pl.ds(pl.multiple_of(y * CH + i * 16, 16), 16), :] = x.astype(BF16)
        return carry

    lax.fori_loop(0, CH // 16, finish, 0)
    gather_start(1, outb)

    def put(i, chunk):
        rows = pl.ds(pl.multiple_of(chunk * CH, CH), CH)
        return pltpu.make_async_copy(outb.at[rows, :], out_h.at[rows, :], oo.at[i])

    put(0, y).start()
    gather_pass(1, outb)
    ag(1, 1, outb).wait_recv()
    put(1, left).start()
    ag(1, 4, outb).wait_recv()
    put(2, right).start()
    ag(1, 2, outb).wait_recv()
    ag(1, 5, outb).wait_recv()
    put(3, opp).start()

    for k in range(1, 5):
        @pl.when(r + 2 * k < REQ)
        def _():
            direct(k).wait_send()

        @pl.when(r >= 2 * (k - 1) + 2 * core)
        def _():
            forward(k - 1, 0).wait_send()

    for i in range(6):
        rs(0, i).wait_send()
        rs(1, i).wait_send()
        ag(0, i, mid).wait_send()
        ag(1, i, outb).wait_send()
    kv_copy.wait()
    for i, chunk in enumerate((y, left, right, opp)):
        put(i, chunk).wait()


def body(tokens, segment_ids, mixer_gain, query_weight, pair_weight, output_weight, feed_gain,
         gate_weight, up_weight, down_weight):
    base, inner = rope_tables()
    hbm = pl.BlockSpec(memory_space=pl.ANY)
    vm = pl.BlockSpec(memory_space=pltpu.VMEM)
    dma = pltpu.SemaphoreType.DMA
    return pl.pallas_call(
        kernel,
        out_shape=(
            jax.ShapeDtypeStruct((T, D), BF16),
            jax.ShapeDtypeStruct((T, 128), BF16),
        ),
        in_specs=[hbm, vm, vm, vm, vm, vm] + [hbm] * 6,
        out_specs=(hbm, hbm),
        scratch_shapes=[
            pltpu.VMEM((T, D), BF16),
            pltpu.VMEM((T, D), BF16),
            pltpu.VMEM((D, 128), BF16),
            pltpu.VMEM((D, C), BF16),
            pltpu.VMEM((C, D), BF16),
            pltpu.VMEM((D, F), BF16),
            pltpu.VMEM((D, F), BF16),
            pltpu.VMEM((F, D), BF16),
            pltpu.VMEM((BLOCKS + 1, KROWS, 128), BF16),
            pltpu.VMEM((BLOCKS + 1, 128, T), BF16),
            pltpu.VMEM(((BLOCKS + 1) * T, 256), BF16),
            pltpu.VMEM((HEADS, T, 128), BF16),
            pltpu.VMEM((HEADS, T, BLOCKS * T), F32),
            pltpu.VMEM((HEADS, T, 128), F32),
            pltpu.VMEM((HEADS * CH, (BLOCKS + 1) * T), BF16),
            pltpu.VMEM((CH, C), BF16),
            pltpu.VMEM((12, CH, HALF), BF16),
            pltpu.VMEM((12, CH, HALF), BF16),
            pltpu.VMEM((CH, D), BF16),
            pltpu.VMEM((CH, D), BF16),
            pltpu.VMEM((CH, D), F32),
            pltpu.VMEM((T, D), BF16),
            pltpu.VMEM((T, D), BF16),
            dma((7,)), dma, dma((4,)),
            dma((4,)), dma((4,)), dma((4,)), dma((4,)),
            dma((12,)), dma((12,)), dma((12,)), dma((12,)),
        ],
        compiler_params=pltpu.CompilerParams(
            collective_id=0, has_side_effects=True, vmem_limit_bytes=64 * 1024 * 1024 - 65536
        ),
        name="block",
    )(
        tokens, segment_ids.reshape(1, T), mixer_gain.reshape(1, D), feed_gain.reshape(1, D),
        jnp.asarray(base), jnp.asarray(inner),
        query_weight, pair_weight, output_weight, gate_weight, up_weight, down_weight,
    )


def solution(mesh):
    return jax.shard_map(
        body,
        mesh=mesh,
        in_specs=(
            P("req", None),
            P("req"),
            P(),
            P(None, "tp"),
            P(None, "tp"),
            P("tp", None),
            P(),
            P(None, "tp"),
            P(None, "tp"),
            P("tp", None),
        ),
        out_specs=(P("req", None), P("req", "tp")),
        check_vma=False,
    )
```
